32 devices in a mesh: groups: 2 (over y), seq: 4 (over z), head: 2 (over x), sub: 2 (over core).
Axes of the slice: x: 2, y: 2, z: 4, core: 2. Of those that a mesh axis runs over, the one named last changes fastest.
Arguments:
- queries: bfloat16 [4608, 8192], P(('groups', 'seq'), ('head', 'sub')), parts along dimension 0, may hold values from -6 to 6
- keys: bfloat16 [4608, 8192], P(('groups', 'seq'), ('head', 'sub')), parts along dimension 0, may hold values from -0.0546875 to 0.0546875
- values: bfloat16 [4608, 8192], P(('groups', 'seq'), ('head', 'sub')), parts along dimension 0, may hold values from -800 to 800
- decay_exp: int32 [64], P(('head', 'sub')), may hold values from 1 to 2303, as said below
- gain: float32 [8192], P(('head', 'sub')), may hold values from 0.5 to 1.5
Outputs:
- normed: bfloat16 [4608, 8192], P(('groups', 'seq'), ('head', 'sub')), parts along dimension 0
- final_state: float32 [128, 128, 128], P(('groups', 'head', 'sub'), 'seq'), parts along dimension 0
The draws below stay inside these ranges and needn't reach their ends.
There are 2 independent parts, one for each index of `groups`. The reference program is written for one: setup_inputs(seed, part) draws one part's arguments, and reference() takes and returns one part's arrays. A program takes and returns all parts, laid end to end along the dimension named above; an argument that names none is the same for every part. Nothing has to cross between parts.
Inputs may be any that keep to these rules, and one draw needn't show every extreme that they name: The decay of head h over one position is 2 ** (-decay_exp[h] / 18432).
All inputs are finite; a program needn't handle non-finite values.
Results may differ from the reference program's by a relative error of at most 0.0049.
Values sent between devices are 32-bit elements; how exact they have to be, the bound alone decides.
A program may use at most 64 MiB of HBM per device.

```python
import jax
import jax.numpy as jnp
from jax import lax

HEADS = 64
DK = 128
TOK_DEV = 576
SEQ_LEN = 2304
N_SEQ = 4
N_HEAD = 2
N_SUB = 2


def draw_values(key, part):
    key_base, key_rows, key_heads = jax.random.split(jax.random.fold_in(key, 11), 3)
    head_shift = jax.random.uniform(key_heads, (HEADS,), jnp.float32)
    head_scale = 10.0 ** ((jnp.arange(HEADS).astype(jnp.float32) + head_shift) / HEADS)
    column_scale = jnp.repeat(head_scale, DK)
    base = jnp.clip(jax.random.normal(key_base, (SEQ_LEN, HEADS * DK), jnp.float32), -4.0, 4.0)
    row_scale = 10.0 ** jax.random.uniform(key_rows, (SEQ_LEN, 1), jnp.float32)
    return (base * row_scale * column_scale[None, :]).astype(jnp.bfloat16)


def draw_decay_exp(key, part):
    key_order, key_slow, key_middle, key_fast = jax.random.split(jax.random.fold_in(key, 23), 4)
    shards = N_HEAD * N_SUB
    per_shard = HEADS // shards
    grouping = jnp.repeat(jax.random.permutation(key_order, shards) % 3, per_shard)
    slow = jax.random.randint(key_slow, (HEADS,), 1, 27)
    middle = jax.random.randint(key_middle, (HEADS,), 27, max(28, SEQ_LEN // 16))
    fast = jax.random.randint(key_fast, (HEADS,), SEQ_LEN // 4, SEQ_LEN)
    return jnp.where(grouping == 0, slow, jnp.where(grouping == 1, middle, fast)).astype(jnp.int32)


def steps_of(rng, shape, pieces, least, high):
    level = 1.0
    for dim, shards_of in pieces:
        draws = jax.random.uniform(jax.random.fold_in(jax.random.fold_in(rng, 6), dim), (shards_of,), jnp.float32, least / len(pieces), high / len(pieces))
        level = level * jnp.repeat(jnp.exp(draws), shape[dim] // shards_of).reshape((-1,) + (1,) * (len(shape) - 1 - dim))
    return level


def gaussian(own_key, dims, deviation, bound, cuts=(), kind=jnp.bfloat16):
    values = deviation * jax.random.normal(own_key, dims, jnp.float32)
    if cuts:
        values = values * steps_of(own_key, dims, cuts, -0.22, 0.18)
    return jnp.clip(values, -bound, bound).astype(kind)


def setup_inputs(seed: int = 0, part: int = 0) -> dict:
    key_list = jax.random.split(jax.random.key(seed), 6)
    own_keys = jax.random.split(jax.random.fold_in(key_list[5], part), 6)
    return {
        "queries": gaussian(own_keys[0], (SEQ_LEN, HEADS * DK), 1.0, 6.0, ((0, 4), (1, 4))),
        "keys": gaussian(own_keys[1], (SEQ_LEN, HEADS * DK), ((DK * TOK_DEV) ** -0.5), 0.0546875, ((0, 4), (1, 4))),
        "values": draw_values(jax.random.fold_in(jax.random.fold_in(key_list[5], part), 71), part),
        "decay_exp": draw_decay_exp(jax.random.fold_in(key_list[5], 71), part),
        "gain": jnp.clip(1.0 + 0.1 * jax.random.normal(key_list[4], (HEADS * DK,), jnp.float32), 0.5, 1.5),
    }


def reference(queries, keys, values, decay_exp, gain):
    decay_rate = decay_exp.astype(jnp.float32) / (8.0 * SEQ_LEN)
    offsets = jnp.arange(TOK_DEV).astype(jnp.float32)
    distance = offsets[:, None] - offsets[None, :]
    causal = distance >= 0
    within = jnp.where(causal[None], jnp.exp2(-decay_rate[:, None, None] * jnp.maximum(distance, 0.0)[None]), 0.0)
    key_decay = jnp.exp2(-decay_rate[None, :] * (TOK_DEV - 1.0 - offsets)[:, None])
    query_decay = jnp.exp2(-decay_rate[None, :] * (offsets + 1.0)[:, None])
    block_decay = jnp.exp2(-decay_rate * TOK_DEV)

    def shaped(array):
        return array.reshape(N_SEQ, TOK_DEV, HEADS, DK)

    def advance(state, blocks):
        query_block, key_block, value_block = blocks
        scores = jnp.einsum('ihd,jhd->hij', query_block.astype(jnp.float32), key_block.astype(jnp.float32), precision=lax.Precision.HIGHEST)
        weights = (scores * within).astype(jnp.bfloat16)
        intra = jnp.einsum('hij,jhd->ihd', weights.astype(jnp.float32), value_block.astype(jnp.float32), precision=lax.Precision.HIGHEST)
        decayed_query = query_block.astype(jnp.float32) * query_decay[:, :, None]
        inter = jnp.einsum('ihd,hde->ihe', decayed_query, state, precision=lax.Precision.HIGHEST)
        scaled_keys = (key_block.astype(jnp.float32) * key_decay[:, :, None]).astype(jnp.bfloat16)
        local_state = jnp.einsum('ihd,ihe->hde', scaled_keys.astype(jnp.float32), value_block.astype(jnp.float32), precision=lax.Precision.HIGHEST)
        return (block_decay[:, None, None] * state + local_state, intra + inter)
    initial = jnp.zeros((HEADS, DK, DK), jnp.float32)
    final_state, mixed = lax.scan(advance, initial, (shaped(queries), shaped(keys), shaped(values)))
    mixed = mixed.reshape(SEQ_LEN, HEADS * DK)
    mean_square = lax.optimization_barrier(jnp.mean(mixed * mixed, axis=1, keepdims=True))
    normed = (mixed * lax.rsqrt(mean_square + 1e-06) * gain[None, :]).astype(jnp.bfloat16)
    return (normed, final_state)
```

```python
import functools

import jax
import jax.numpy as jnp
from jax import lax
from jax.experimental import pallas as pl
from jax.experimental.pallas import tpu as pltpu
from jax.sharding import PartitionSpec as P

MESH = pl.DeviceIdType.MESH
F32 = jnp.float32
BF16 = jnp.bfloat16
PIECES = 2
ROW_BLOCK = 192


def dot(a, b, dims):
    return lax.dot_general(a, b, (dims, ((), ())), preferred_element_type=F32)


def mix_kernel(
    n_seq, n_head, n_sub, heads, dk,
    exps, q_hbm, k_hbm, v_hbm,
    mixed_hbm, inv_hbm, final_hbm,
    q_buf, k_buf, v_buf, mix, held, outgoing, final_rows, squares, sums, inv,
    in_sem, out_sem, send_sem, recv_sem, fin_send, fin_recv, sum_send, sum_recv, tail_sem,
):
    tokens = q_buf.shape[0]
    padded = squares.shape[0]
    rows = dk // n_seq
    part = dk // PIECES
    seq = lax.axis_index("seq")
    last = n_seq - 1
    n_group = n_head * n_sub
    here = lax.axis_index("head") * n_sub + lax.axis_index("sub")

    barrier = pltpu.get_barrier_semaphore()
    for step in range(1, n_seq):
        pl.semaphore_signal(
            barrier, inc=1, device_id={"seq": lax.rem(seq + step, n_seq)}, device_id_type=MESH
        )
    for step in range(1, n_group):
        there = lax.rem(here + step, n_group)
        pl.semaphore_signal(
            barrier, inc=1,
            device_id={"head": there // n_sub, "sub": lax.rem(there, n_sub)},
            device_id_type=MESH,
        )

    def columns(h):
        return pl.ds(pl.multiple_of(h * dk, dk), dk)

    def load(h, slot):
        hbm, buf = ((k_hbm, k_buf), (v_hbm, v_buf), (q_hbm, q_buf))[slot]
        return pltpu.make_async_copy(hbm.at[:, columns(h)], buf.at[:, columns(h)], in_sem.at[slot, h])

    def store(h):
        return pltpu.make_async_copy(mix.at[:, columns(h)], mixed_hbm.at[:, columns(h)], out_sem.at[h])

    def piece(h, p):
        span = pl.ds(p * part, part)
        return pltpu.make_async_remote_copy(
            src_ref=outgoing.at[h, span], dst_ref=held.at[h, span],
            send_sem=send_sem.at[h, p], recv_sem=recv_sem.at[h, p],
            device_id={"seq": lax.rem(seq + 1, n_seq)}, device_id_type=MESH,
        )

    def start_loads(h, carry):
        for slot in range(3):
            load(h, slot).start()
        return carry

    lax.fori_loop(0, heads, start_loads, 0)

    @pl.when(seq == 0)
    def _():
        held[...] = jnp.zeros_like(held)

    squares[...] = jnp.zeros_like(squares)
    position = lax.broadcasted_iota(jnp.int32, (tokens, dk), 0).astype(F32)
    pl.semaphore_wait(barrier, n_seq - 1 + n_group - 1)

    def head_step(h, carry):
        cols = columns(h)
        rate = jnp.full((1, dk), exps[h], jnp.int32).astype(F32) / (8.0 * tokens * n_seq)
        load(h, 0).wait()
        load(h, 1).wait()
        scaled = (v_buf[:, cols].astype(F32) * jnp.exp2(position * rate)).astype(BF16)
        v_buf[:, cols] = scaled
        outgoing[h] = dot(k_buf[:, cols], scaled, ((0,), (0,))) * jnp.exp2(-rate * (tokens - 1.0))

        @pl.when(seq == 0)
        def _():
            for p in range(PIECES):
                piece(h, p).start()

        load(h, 2).wait()
        block = ROW_BLOCK if tokens % ROW_BLOCK == 0 else tokens
        lower = lax.broadcasted_iota(jnp.int32, (block, block), 0) >= lax.broadcasted_iota(
            jnp.int32, (block, block), 1
        )
        for top in range(0, tokens, block):
            q_rows = q_buf[top : top + block, cols]
            diagonal = dot(q_rows, k_buf[top : top + block, cols], ((1,), (1,)))
            weights = jnp.where(lower, diagonal, 0.0).astype(BF16)
            total = dot(weights, v_buf[top : top + block, cols], ((1,), (0,)))
            if top:
                before = dot(q_rows, k_buf[:top, cols], ((1,), (1,))).astype(BF16)
                total += dot(before, v_buf[:top, cols], ((1,), (0,)))
            mix[top : top + block, cols] = total

        block_decay = jnp.exp2(-rate * tokens)

        @pl.when(seq > 0)
        def _():
            for p in range(PIECES):
                span = pl.ds(p * part, part)
                piece(h, p).wait_recv()
                outgoing[h, span] = outgoing[h, span] + held[h, span] * block_decay

                @pl.when(seq < last)
                def _():
                    piece(h, p).start()

        @pl.when(seq == last)
        def _():
            for b in range(n_seq):
                final_rows[b, h] = outgoing[h, b * rows : (b + 1) * rows]
            for b in range(last):
                pltpu.make_async_remote_copy(
                    src_ref=final_rows.at[b, h], dst_ref=final_hbm.at[h],
                    send_sem=fin_send, recv_sem=fin_recv,
                    device_id={"seq": b}, device_id_type=MESH,
                ).start()

        state = (held[h] * jnp.exp2(-rate)).astype(BF16)
        inter = dot(q_buf[:, cols], state, ((1,), (0,)))
        mixed = (mix[:, cols] + inter) * jnp.exp2(-(position * rate))
        mix[:, cols] = mixed
        squares[:tokens] += mixed * mixed
        store(h).start()
        return carry

    lax.fori_loop(0, heads, head_step, 0)

    sums[here] = jnp.broadcast_to(
        jnp.sum(squares[...].T, axis=0, keepdims=True), (8, padded)
    )

    def sum_copy(step, slot, target):
        return pltpu.make_async_remote_copy(
            src_ref=sums.at[slot], dst_ref=sums.at[slot],
            send_sem=sum_send.at[step], recv_sem=sum_recv.at[step],
            device_id={"head": target // n_sub, "sub": lax.rem(target, n_sub)},
            device_id_type=MESH,
        )

    for step in range(1, n_group):
        sum_copy(step, here, lax.rem(here + step, n_group)).start()
    for step in range(1, n_group):
        source = lax.rem(here - step + n_group, n_group)
        sum_copy(step, source, source).wait_recv()
    total = sums[0]
    for slot in range(1, n_group):
        total += sums[slot]
    factor = lax.rsqrt(total / (heads * dk * n_group) + 1e-06)
    inv[...] = jnp.broadcast_to(factor[:1], (dk, padded)).T[:tokens]
    inv_copy = pltpu.make_async_copy(inv, inv_hbm, tail_sem.at[0])
    inv_copy.start()

    @pl.when(seq == last)
    def _():
        own = pltpu.make_async_copy(final_rows.at[last], final_hbm, tail_sem.at[1])
        own.start()
        sent = final_rows.at[pl.ds(0, last)]
        pltpu.make_async_copy(sent, sent, fin_send).wait()
        own.wait()

    @pl.when(seq < last)
    def _():
        pltpu.make_async_copy(final_hbm, final_hbm, fin_recv).wait()

        def finish(h, carry):
            for p in range(PIECES):
                piece(h, p).wait_send()
            return carry

        lax.fori_loop(0, heads, finish, 0)

    for step in range(1, n_group):
        sum_copy(step, here, lax.rem(here + step, n_group)).wait_send()

    def stored(h, carry):
        store(h).wait()
        return carry

    lax.fori_loop(0, heads, stored, 0)
    inv_copy.wait()


def local(n_seq, n_head, n_sub, queries, keys, values, decay_exp, gain):
    tokens, features = queries.shape
    heads = decay_exp.shape[0]
    dk = features // heads
    rows = dk // n_seq
    padded = -(-tokens // 128) * 128
    n_group = n_head * n_sub
    hbm = pl.BlockSpec(memory_space=pl.ANY)
    mixed, inv, final = pl.pallas_call(
        functools.partial(mix_kernel, n_seq, n_head, n_sub, heads, dk),
        out_shape=(
            jax.ShapeDtypeStruct((tokens, features), F32),
            jax.ShapeDtypeStruct((tokens, dk), F32),
            jax.ShapeDtypeStruct((heads, rows, dk), F32),
        ),
        in_specs=[pl.BlockSpec(memory_space=pltpu.SMEM)] + [pl.BlockSpec(memory_space=pltpu.HBM)] * 3,
        out_specs=(hbm, hbm, hbm),
        scratch_shapes=[
            pltpu.VMEM((tokens, features), BF16),
            pltpu.VMEM((tokens, features), BF16),
            pltpu.VMEM((tokens, features), BF16),
            pltpu.VMEM((tokens, features), F32),
            pltpu.VMEM((heads, dk, dk), F32),
            pltpu.VMEM((heads, dk, dk), F32),
            pltpu.VMEM((n_seq, heads, rows, dk), F32),
            pltpu.VMEM((padded, dk), F32),
            pltpu.VMEM((n_group, 8, padded), F32),
            pltpu.VMEM((tokens, dk), F32),
            pltpu.SemaphoreType.DMA((3, heads)),
            pltpu.SemaphoreType.DMA((heads,)),
            pltpu.SemaphoreType.DMA((heads, PIECES)),
            pltpu.SemaphoreType.DMA((heads, PIECES)),
            pltpu.SemaphoreType.DMA,
            pltpu.SemaphoreType.DMA,
            pltpu.SemaphoreType.DMA((n_group,)),
            pltpu.SemaphoreType.DMA((n_group,)),
            pltpu.SemaphoreType.DMA((2,)),
        ],
        compiler_params=pltpu.CompilerParams(
            collective_id=0, has_side_effects=True, vmem_limit_bytes=40 * 1024 * 1024
        ),
        name="mix",
    )(decay_exp, queries, keys, values)
    normed = (mixed * inv[:, :1] * gain[None, :]).astype(BF16)
    return normed, final


def solution(mesh):
    return jax.shard_map(
        functools.partial(local, mesh.shape["seq"], mesh.shape["head"], mesh.shape["sub"]),
        mesh=mesh,
        in_specs=(
            P(("groups", "seq"), ("head", "sub")),
            P(("groups", "seq"), ("head", "sub")),
            P(("groups", "seq"), ("head", "sub")),
            P(("head", "sub")),
            P(("head", "sub")),
        ),
        out_specs=(
            P(("groups", "seq"), ("head", "sub")),
            P(("groups", "head", "sub"), "seq", None),
        ),
        check_vma=False,
    )
```

```python
import functools

import jax
import jax.numpy as jnp
from jax import lax
from jax.experimental import pallas as pl
from jax.experimental.pallas import tpu as pltpu
from jax.sharding import PartitionSpec as P

MESH = pl.DeviceIdType.MESH
F32 = jnp.float32
BF16 = jnp.bfloat16
PIECES = 2
ROW_BLOCK = 192


def dot(a, b, dims):
    return lax.dot_general(a, b, (dims, ((), ())), preferred_element_type=F32)


def mix_kernel(
    n_seq, n_head, n_sub, heads, dk,
    exps, q_hbm, k_hbm, v_hbm,
    mixed_hbm, inv_hbm, final_hbm,
    q_buf, k_buf, v_buf, mix, held, outgoing, final_rows, squares, sums, inv, running, late, final,
    in_sem, out_sem, send_sem, recv_sem, fin_send, fin_recv, sum_send, sum_recv, tail_sem,
):
    tokens = q_buf.shape[0]
    padded = squares.shape[0]
    rows = dk // n_seq
    part = dk // PIECES
    seq = lax.axis_index("seq")
    last = n_seq - 1
    n_group = n_head * n_sub
    here = lax.axis_index("head") * n_sub + lax.axis_index("sub")

    barrier = pltpu.get_barrier_semaphore()
    for step in range(1, n_seq):
        pl.semaphore_signal(
            barrier, inc=1, device_id={"seq": lax.rem(seq + step, n_seq)}, device_id_type=MESH
        )
    for step in range(1, n_group):
        there = lax.rem(here + step, n_group)
        pl.semaphore_signal(
            barrier, inc=1,
            device_id={"head": there // n_sub, "sub": lax.rem(there, n_sub)},
            device_id_type=MESH,
        )

    def columns(h):
        return pl.ds(pl.multiple_of(h * dk, dk), dk)

    def load(h, slot):
        hbm, buf = ((k_hbm, k_buf), (v_hbm, v_buf), (q_hbm, q_buf))[slot]
        return pltpu.make_async_copy(hbm.at[:, columns(h)], buf.at[:, columns(h)], in_sem.at[slot, h])

    def store(h):
        return pltpu.make_async_copy(mix.at[:, columns(h)], mixed_hbm.at[:, columns(h)], out_sem.at[h])

    def piece(h, p):
        span = pl.ds(p * part, part)
        return pltpu.make_async_remote_copy(
            src_ref=outgoing.at[h, span], dst_ref=held.at[h, span],
            send_sem=send_sem.at[h, p], recv_sem=recv_sem.at[h, p],
            device_id={"seq": lax.rem(seq + 1, n_seq)}, device_id_type=MESH,
        )

    def start_loads(h, carry):
        for slot in range(3):
            load(h, slot).start()
        return carry

    lax.fori_loop(0, heads, start_loads, 0)

    @pl.when(seq == 0)
    def _():
        held[...] = jnp.zeros_like(held)

    squares[...] = jnp.zeros_like(squares)
    position = lax.broadcasted_iota(jnp.int32, (tokens, dk), 0).astype(F32)
    pl.semaphore_wait(barrier, n_seq - 1 + n_group - 1)

    def head_step(h, carry):
        cols = columns(h)
        rate = jnp.full((1, dk), exps[h], jnp.int32).astype(F32) / (8.0 * tokens * n_seq)
        load(h, 0).wait()
        load(h, 1).wait()
        block = ROW_BLOCK if tokens % ROW_BLOCK == 0 else tokens
        tops = range(0, tokens, block)
        state = jnp.zeros((dk, dk), F32)
        for c, top in enumerate(tops):
            span = slice(top, top + block)
            scaled = (v_buf[span, cols].astype(F32) * jnp.exp2(position[span] * rate)).astype(BF16)
            v_buf[span, cols] = scaled
            running[c] = state
            state += dot(k_buf[span, cols], scaled, ((0,), (0,)))
        own = state * jnp.exp2(-rate * (tokens - 1.0))
        outgoing[h] = own
        for b in range(n_seq):
            final_rows[b, h] = own[b * rows : (b + 1) * rows]

        @pl.when(seq == 0)
        def _():
            for p in range(PIECES):
                piece(h, p).start()

        for b in range(last):

            @pl.when(b < seq)
            def _():
                pltpu.make_async_remote_copy(
                    src_ref=final_rows.at[b, h], dst_ref=late.at[seq, h],
                    send_sem=fin_send.at[b], recv_sem=fin_recv.at[seq],
                    device_id={"seq": b}, device_id_type=MESH,
                ).start()

        load(h, 2).wait()
        lower = lax.broadcasted_iota(jnp.int32, (block, block), 0) >= lax.broadcasted_iota(
            jnp.int32, (block, block), 1
        )
        for top in tops:
            span = slice(top, top + block)
            scores = dot(q_buf[span, cols], k_buf[span, cols], ((1,), (1,)))
            weights = jnp.where(lower, scores, 0.0).astype(BF16)
            mix[span, cols] = dot(weights, v_buf[span, cols], ((1,), (0,)))

        block_decay = jnp.exp2(-rate * tokens)

        @pl.when(seq > 0)
        def _():
            for p in range(PIECES):
                span = pl.ds(p * part, part)
                piece(h, p).wait_recv()

                @pl.when(seq < last)
                def _():
                    outgoing[h, span] = outgoing[h, span] + held[h, span] * block_decay
                    piece(h, p).start()

        start = held[h] * jnp.exp2(-rate)
        for c, top in enumerate(tops):
            span = slice(top, top + block)
            inter = dot(q_buf[span, cols], (start + running[c]).astype(BF16), ((1,), (0,)))
            mixed = (mix[span, cols] + inter) * jnp.exp2(-(position[span] * rate))
            mix[span, cols] = mixed
            squares[span] += mixed * mixed
        store(h).start()
        return carry

    lax.fori_loop(0, heads, head_step, 0)

    sums[here] = jnp.broadcast_to(
        jnp.sum(squares[...].T, axis=0, keepdims=True), (8, padded)
    )

    def sum_copy(step, slot, target):
        return pltpu.make_async_remote_copy(
            src_ref=sums.at[slot], dst_ref=sums.at[slot],
            send_sem=sum_send.at[step], recv_sem=sum_recv.at[step],
            device_id={"head": target // n_sub, "sub": lax.rem(target, n_sub)},
            device_id_type=MESH,
        )

    for step in range(1, n_group):
        sum_copy(step, here, lax.rem(here + step, n_group)).start()
    for b in range(n_seq):

        @pl.when(seq == b)
        def _():
            for m in range(b + 1, n_seq):
                pltpu.make_async_copy(late.at[m], late.at[m], fin_recv.at[m]).wait()

            def finals(h, carry):
                rate = jnp.full((1, dk), exps[h], jnp.int32).astype(F32) / (8.0 * n_seq)
                total = held[h, b * rows : (b + 1) * rows] * jnp.exp2(-rate * (n_seq - b))
                total += final_rows[b, h] * jnp.exp2(-rate * (last - b))
                for m in range(b + 1, n_seq):
                    total += late[m, h] * jnp.exp2(-rate * (last - m))
                final[h] = total
                return carry

            lax.fori_loop(0, heads, finals, 0)

    final_copy = pltpu.make_async_copy(final, final_hbm, tail_sem.at[1])
    final_copy.start()
    for step in range(1, n_group):
        source = lax.rem(here - step + n_group, n_group)
        sum_copy(step, source, source).wait_recv()
    total = sums[0]
    for slot in range(1, n_group):
        total += sums[slot]
    factor = lax.rsqrt(total / (heads * dk * n_group) + 1e-06)
    inv[...] = jnp.broadcast_to(factor[:1], (dk, padded)).T[:tokens]
    inv_copy = pltpu.make_async_copy(inv, inv_hbm, tail_sem.at[0])
    inv_copy.start()

    for b in range(last):

        @pl.when(b < seq)
        def _():
            pltpu.make_async_copy(final_rows.at[b], final_rows.at[b], fin_send.at[b]).wait()

    @pl.when(seq < last)
    def _():
        def finish(h, carry):
            for p in range(PIECES):
                piece(h, p).wait_send()
            return carry

        lax.fori_loop(0, heads, finish, 0)

    for step in range(1, n_group):
        sum_copy(step, here, lax.rem(here + step, n_group)).wait_send()

    def stored(h, carry):
        store(h).wait()
        return carry

    lax.fori_loop(0, heads, stored, 0)
    inv_copy.wait()
    final_copy.wait()


def local(n_seq, n_head, n_sub, queries, keys, values, decay_exp, gain):
    tokens, features = queries.shape
    heads = decay_exp.shape[0]
    dk = features // heads
    rows = dk // n_seq
    padded = -(-tokens // 128) * 128
    n_group = n_head * n_sub
    hbm = pl.BlockSpec(memory_space=pl.ANY)
    mixed, inv, final = pl.pallas_call(
        functools.partial(mix_kernel, n_seq, n_head, n_sub, heads, dk),
        out_shape=(
            jax.ShapeDtypeStruct((tokens, features), F32),
            jax.ShapeDtypeStruct((tokens, dk), F32),
            jax.ShapeDtypeStruct((heads, rows, dk), F32),
        ),
        in_specs=[pl.BlockSpec(memory_space=pltpu.SMEM)] + [pl.BlockSpec(memory_space=pltpu.HBM)] * 3,
        out_specs=(hbm, hbm, hbm),
        scratch_shapes=[
            pltpu.VMEM((tokens, features), BF16),
            pltpu.VMEM((tokens, features), BF16),
            pltpu.VMEM((tokens, features), BF16),
            pltpu.VMEM((tokens, features), F32),
            pltpu.VMEM((heads, dk, dk), F32),
            pltpu.VMEM((heads, dk, dk), F32),
            pltpu.VMEM((n_seq, heads, rows, dk), F32),
            pltpu.VMEM((padded, dk), F32),
            pltpu.VMEM((n_group, 8, padded), F32),
            pltpu.VMEM((tokens, dk), F32),
            pltpu.VMEM((max(1, tokens // ROW_BLOCK), dk, dk), F32),
            pltpu.VMEM((n_seq, heads, rows, dk), F32),
            pltpu.VMEM((heads, rows, dk), F32),
            pltpu.SemaphoreType.DMA((3, heads)),
            pltpu.SemaphoreType.DMA((heads,)),
            pltpu.SemaphoreType.DMA((heads, PIECES)),
            pltpu.SemaphoreType.DMA((heads, PIECES)),
            pltpu.SemaphoreType.DMA((n_seq,)),
            pltpu.SemaphoreType.DMA((n_seq,)),
            pltpu.SemaphoreType.DMA((n_group,)),
            pltpu.SemaphoreType.DMA((n_group,)),
            pltpu.SemaphoreType.DMA((2,)),
        ],
        compiler_params=pltpu.CompilerParams(
            collective_id=0, has_side_effects=True, vmem_limit_bytes=40 * 1024 * 1024
        ),
        name="mix",
    )(decay_exp, *(pltpu.with_memory_space_constraint(x, pltpu.HBM) for x in (queries, keys, values)))
    normed = (mixed * inv[:, :1] * gain[None, :]).astype(BF16)
    return normed, final


def solution(mesh):
    return jax.shard_map(
        functools.partial(local, mesh.shape["seq"], mesh.shape["head"], mesh.shape["sub"]),
        mesh=mesh,
        in_specs=(
            P(("groups", "seq"), ("head", "sub")),
            P(("groups", "seq"), ("head", "sub")),
            P(("groups", "seq"), ("head", "sub")),
            P(("head", "sub")),
            P(("head", "sub")),
        ),
        out_specs=(
            P(("groups", "seq"), ("head", "sub")),
            P(("groups", "head", "sub"), "seq", None),
        ),
        check_vma=False,
    )
```

```python
import functools

import jax
import jax.numpy as jnp
from jax import lax
from jax.experimental import pallas as pl
from jax.experimental.pallas import tpu as pltpu
from jax.sharding import PartitionSpec as P

MESH = pl.DeviceIdType.MESH
F32 = jnp.float32
BF16 = jnp.bfloat16
PIECES = 2
NORM_VMEM = 16
LEAD = 3
ROW_BLOCK = 192


def dot(a, b, dims):
    return lax.dot_general(a, b, (dims, ((), ())), preferred_element_type=F32)


def mix_kernel(
    n_seq, n_head, n_sub, heads, dk,
    exps, q_hbm, k_hbm, v_hbm,
    mixed_hbm, inv_hbm, final_hbm,
    q_buf, k_buf, v_buf, mix, held, outgoing, final_rows, squares, sums, inv, running, late, final,
    in_sem, out_sem, send_sem, recv_sem, fin_send, fin_recv, sum_send, sum_recv, tail_sem,
):
    tokens = q_buf.shape[0]
    padded = squares.shape[0]
    rows = dk // n_seq
    part = dk // PIECES
    seq = lax.axis_index("seq")
    last = n_seq - 1
    n_group = n_head * n_sub
    here = lax.axis_index("head") * n_sub + lax.axis_index("sub")

    barrier = pltpu.get_barrier_semaphore()
    for step in range(1, n_seq):
        pl.semaphore_signal(
            barrier, inc=1, device_id={"seq": lax.rem(seq + step, n_seq)}, device_id_type=MESH
        )
    for step in range(1, n_group):
        there = lax.rem(here + step, n_group)
        pl.semaphore_signal(
            barrier, inc=1,
            device_id={"head": there // n_sub, "sub": lax.rem(there, n_sub)},
            device_id_type=MESH,
        )

    def columns(h):
        return pl.ds(pl.multiple_of(h * dk, dk), dk)

    def load(h, slot):
        hbm, buf = ((k_hbm, k_buf), (v_hbm, v_buf), (q_hbm, q_buf))[slot]
        return pltpu.make_async_copy(hbm.at[:, columns(h)], buf.at[:, columns(h)], in_sem.at[slot, h])

    def store(h):
        return pltpu.make_async_copy(mix.at[:, columns(h)], mixed_hbm.at[:, columns(h)], out_sem.at[h])

    def piece(h, p):
        span = pl.ds(p * part, part)
        return pltpu.make_async_remote_copy(
            src_ref=outgoing.at[h, span], dst_ref=held.at[h, span],
            send_sem=send_sem.at[h, p], recv_sem=recv_sem.at[h, p],
            device_id={"seq": lax.rem(seq + 1, n_seq)}, device_id_type=MESH,
        )

    def start_loads(h, carry):
        for slot in range(3):
            load(h, slot).start()
        return carry

    lax.fori_loop(0, heads, start_loads, 0)

    @pl.when(seq == 0)
    def _():
        held[...] = jnp.zeros_like(held)

    squares[...] = jnp.zeros_like(squares)
    position = lax.broadcasted_iota(jnp.int32, (tokens, dk), 0).astype(F32)
    pl.semaphore_wait(barrier, n_seq - 1 + n_group - 1)

    block = ROW_BLOCK if tokens % ROW_BLOCK == 0 else tokens
    tops = range(0, tokens, block)

    def prepare(h, carry):
        cols = columns(h)
        rate = jnp.full((1, dk), exps[h], jnp.int32).astype(F32) / (8.0 * tokens * n_seq)
        load(h, 0).wait()
        load(h, 1).wait()
        state = jnp.zeros((dk, dk), F32)
        for c, top in enumerate(tops):
            span = slice(top, top + block)
            scaled = (v_buf[span, cols].astype(F32) * jnp.exp2(position[span] * rate)).astype(BF16)
            v_buf[span, cols] = scaled
            running[h, c] = state
            state += dot(k_buf[span, cols], scaled, ((0,), (0,)))
        own = state * jnp.exp2(-rate * (tokens - 1.0))
        outgoing[h] = own
        for b in range(n_seq):
            final_rows[b, h] = own[b * rows : (b + 1) * rows]

        @pl.when(seq == 0)
        def _():
            for p in range(PIECES):
                piece(h, p).start()

        for b in range(last):

            @pl.when(b < seq)
            def _():
                pltpu.make_async_remote_copy(
                    src_ref=final_rows.at[b, h], dst_ref=late.at[seq, h],
                    send_sem=fin_send.at[b], recv_sem=fin_recv.at[seq],
                    device_id={"seq": b}, device_id_type=MESH,
                ).start()

        load(h, 2).wait()
        lower = lax.broadcasted_iota(jnp.int32, (block, block), 0) >= lax.broadcasted_iota(
            jnp.int32, (block, block), 1
        )
        for top in tops:
            span = slice(top, top + block)
            scores = dot(q_buf[span, cols], k_buf[span, cols], ((1,), (1,)))
            weights = jnp.where(lower, scores, 0.0).astype(BF16)
            mix[span, cols] = dot(weights, v_buf[span, cols], ((1,), (0,)))
        return carry

    def head_step(h, carry):
        cols = columns(h)
        rate = jnp.full((1, dk), exps[h], jnp.int32).astype(F32) / (8.0 * tokens * n_seq)
        block_decay = jnp.exp2(-rate * tokens)

        @pl.when(seq > 0)
        def _():
            for p in range(PIECES):
                span = pl.ds(p * part, part)
                piece(h, p).wait_recv()

                @pl.when(seq < last)
                def _():
                    outgoing[h, span] = outgoing[h, span] + held[h, span] * block_decay
                    piece(h, p).start()

        start = held[h] * jnp.exp2(-rate)
        for c, top in enumerate(tops):
            span = slice(top, top + block)
            inter = dot(q_buf[span, cols], (start + running[h, c]).astype(BF16), ((1,), (0,)))
            mixed = (mix[span, cols] + inter) * jnp.exp2(-(position[span] * rate))
            mix[span, cols] = mixed
            squares[span] += mixed * mixed
        store(h).start()

        @pl.when(h + lead < heads)
        def _():
            prepare(h + lead, 0)

        return carry

    lead = jnp.minimum(1 + LEAD * seq, heads)
    lax.fori_loop(0, lead, prepare, 0)
    lax.fori_loop(0, heads, head_step, 0)

    sums[here] = jnp.broadcast_to(
        jnp.sum(squares[...].T, axis=0, keepdims=True), (8, padded)
    )

    def sum_copy(step, slot, target):
        return pltpu.make_async_remote_copy(
            src_ref=sums.at[slot], dst_ref=sums.at[slot],
            send_sem=sum_send.at[step], recv_sem=sum_recv.at[step],
            device_id={"head": target // n_sub, "sub": lax.rem(target, n_sub)},
            device_id_type=MESH,
        )

    for step in range(1, n_group):
        sum_copy(step, here, lax.rem(here + step, n_group)).start()
    for b in range(n_seq):

        @pl.when(seq == b)
        def _():
            for m in range(b + 1, n_seq):
                pltpu.make_async_copy(late.at[m], late.at[m], fin_recv.at[m]).wait()

            def finals(h, carry):
                rate = jnp.full((1, dk), exps[h], jnp.int32).astype(F32) / (8.0 * n_seq)
                total = held[h, b * rows : (b + 1) * rows] * jnp.exp2(-rate * (n_seq - b))
                total += final_rows[b, h] * jnp.exp2(-rate * (last - b))
                for m in range(b + 1, n_seq):
                    total += late[m, h] * jnp.exp2(-rate * (last - m))
                final[h] = total
                return carry

            lax.fori_loop(0, heads, finals, 0)

    final_copy = pltpu.make_async_copy(final, final_hbm, tail_sem.at[1])
    final_copy.start()
    for step in range(1, n_group):
        source = lax.rem(here - step + n_group, n_group)
        sum_copy(step, source, source).wait_recv()
    total = sums[0]
    for slot in range(1, n_group):
        total += sums[slot]
    factor = lax.rsqrt(total / (heads * dk * n_group) + 1e-06)
    inv[...] = jnp.broadcast_to(factor[:1], (dk, padded)).T[:tokens]
    inv_copy = pltpu.make_async_copy(inv, inv_hbm, tail_sem.at[0])
    inv_copy.start()

    for b in range(last):

        @pl.when(b < seq)
        def _():
            pltpu.make_async_copy(final_rows.at[b], final_rows.at[b], fin_send.at[b]).wait()

    @pl.when(seq < last)
    def _():
        def finish(h, carry):
            for p in range(PIECES):
                piece(h, p).wait_send()
            return carry

        lax.fori_loop(0, heads, finish, 0)

    for step in range(1, n_group):
        sum_copy(step, here, lax.rem(here + step, n_group)).wait_send()

    def stored(h, carry):
        store(h).wait()
        return carry

    lax.fori_loop(0, heads, stored, 0)
    inv_copy.wait()
    final_copy.wait()


def norm_kernel(heads, dk, mixed, inv, final, gain, normed_hbm, final_hbm, normed, sems):
    final_copy = pltpu.make_async_copy(final, final_hbm, sems.at[heads])
    final_copy.start()

    def columns(h):
        return pl.ds(pl.multiple_of(h * dk, dk), dk)

    def copy(h):
        return pltpu.make_async_copy(normed.at[:, columns(h)], normed_hbm.at[:, columns(h)], sems.at[h])

    def scale(h, carry):
        cols = columns(h)
        normed[:, cols] = (mixed[:, cols] * inv[...] * gain[:, cols]).astype(BF16)
        copy(h).start()
        return carry

    def finish(h, carry):
        copy(h).wait()
        return carry

    lax.fori_loop(0, heads, scale, 0)
    lax.fori_loop(0, heads, finish, 0)
    final_copy.wait()


def local(n_seq, n_head, n_sub, queries, keys, values, decay_exp, gain):
    tokens, features = queries.shape
    heads = decay_exp.shape[0]
    dk = features // heads
    rows = dk // n_seq
    padded = -(-tokens // 128) * 128
    n_group = n_head * n_sub
    hbm = pl.BlockSpec(memory_space=pl.ANY)
    mixed, inv, final = pl.pallas_call(
        functools.partial(mix_kernel, n_seq, n_head, n_sub, heads, dk),
        out_shape=(
            jax.ShapeDtypeStruct((tokens, features), F32),
            jax.ShapeDtypeStruct((tokens, dk), F32),
            jax.ShapeDtypeStruct((heads, rows, dk), F32),
        ),
        in_specs=[pl.BlockSpec(memory_space=pltpu.SMEM)] + [pl.BlockSpec(memory_space=pltpu.HBM)] * 3,
        out_specs=(hbm, hbm, hbm),
        scratch_shapes=[
            pltpu.VMEM((tokens, features), BF16),
            pltpu.VMEM((tokens, features), BF16),
            pltpu.VMEM((tokens, features), BF16),
            pltpu.VMEM((tokens, features), F32),
            pltpu.VMEM((heads, dk, dk), F32),
            pltpu.VMEM((heads, dk, dk), F32),
            pltpu.VMEM((n_seq, heads, rows, dk), F32),
            pltpu.VMEM((padded, dk), F32),
            pltpu.VMEM((n_group, 8, padded), F32),
            pltpu.VMEM((tokens, dk), F32),
            pltpu.VMEM((heads, max(1, tokens // ROW_BLOCK), dk, dk), F32),
            pltpu.VMEM((n_seq, heads, rows, dk), F32),
            pltpu.VMEM((heads, rows, dk), F32),
            pltpu.SemaphoreType.DMA((3, heads)),
            pltpu.SemaphoreType.DMA((heads,)),
            pltpu.SemaphoreType.DMA((heads, PIECES)),
            pltpu.SemaphoreType.DMA((heads, PIECES)),
            pltpu.SemaphoreType.DMA((n_seq,)),
            pltpu.SemaphoreType.DMA((n_seq,)),
            pltpu.SemaphoreType.DMA((n_group,)),
            pltpu.SemaphoreType.DMA((n_group,)),
            pltpu.SemaphoreType.DMA((2,)),
        ],
        compiler_params=pltpu.CompilerParams(
            collective_id=0, has_side_effects=True, vmem_limit_bytes=40 * 1024 * 1024
        ),
        name="mix",
    )(*(pltpu.with_memory_space_constraint(x, pltpu.HBM) for x in (decay_exp, queries, keys, values)))
    vmem = pl.BlockSpec(memory_space=pltpu.VMEM)
    return pl.pallas_call(
        functools.partial(norm_kernel, heads, dk),
        out_shape=(
            jax.ShapeDtypeStruct((tokens, features), BF16),
            jax.ShapeDtypeStruct((heads, rows, dk), F32),
        ),
        in_specs=[vmem] * 4,
        out_specs=(pl.BlockSpec(memory_space=pltpu.HBM),) * 2,
        scratch_shapes=[
            pltpu.VMEM((tokens, features), BF16),
            pltpu.SemaphoreType.DMA((heads + 1,)),
        ],
        compiler_params=pltpu.CompilerParams(vmem_limit_bytes=NORM_VMEM * 1024 * 1024),
        name="norm",
    )(
        *(pltpu.with_memory_space_constraint(x, pltpu.VMEM) for x in (mixed, inv, final)),
        gain.reshape(1, features),
    )


def solution(mesh):
    return jax.shard_map(
        functools.partial(local, mesh.shape["seq"], mesh.shape["head"], mesh.shape["sub"]),
        mesh=mesh,
        in_specs=(
            P(("groups", "seq"), ("head", "sub")),
            P(("groups", "seq"), ("head", "sub")),
            P(("groups", "seq"), ("head", "sub")),
            P(("head", "sub")),
            P(("head", "sub")),
        ),
        out_specs=(
            P(("groups", "seq"), ("head", "sub")),
            P(("groups", "head", "sub"), "seq", None),
        ),
        check_vma=False,
    )
```

```python
import functools

import jax
import jax.numpy as jnp
from jax import lax
from jax.experimental import pallas as pl
from jax.experimental.pallas import tpu as pltpu
from jax.sharding import PartitionSpec as P

MESH = pl.DeviceIdType.MESH
F32 = jnp.float32
BF16 = jnp.bfloat16
PIECES = 2
NORM_ROWS = 96
NORM_VMEM = 16
LEAD = 3
ROW_BLOCK = 192


def dot(a, b, dims):
    return lax.dot_general(a, b, (dims, ((), ())), preferred_element_type=F32)


def mix_kernel(
    n_seq, n_head, n_sub, heads, dk,
    exps, q_hbm, k_hbm, v_hbm,
    mixed_hbm, inv_hbm, final_hbm,
    q_buf, k_buf, v_buf, mix, held, outgoing, final_rows, squares, sums, inv, running, late, final,
    in_sem, out_sem, send_sem, recv_sem, fin_send, fin_recv, sum_send, sum_recv, tail_sem,
):
    tokens = q_buf.shape[0]
    padded = squares.shape[0]
    rows = dk // n_seq
    part = dk // PIECES
    seq = lax.axis_index("seq")
    last = n_seq - 1
    n_group = n_head * n_sub
    here = lax.axis_index("head") * n_sub + lax.axis_index("sub")

    barrier = pltpu.get_barrier_semaphore()
    for step in range(1, n_seq):
        pl.semaphore_signal(
            barrier, inc=1, device_id={"seq": lax.rem(seq + step, n_seq)}, device_id_type=MESH
        )
    for step in range(1, n_group):
        there = lax.rem(here + step, n_group)
        pl.semaphore_signal(
            barrier, inc=1,
            device_id={"head": there // n_sub, "sub": lax.rem(there, n_sub)},
            device_id_type=MESH,
        )

    def columns(h):
        return pl.ds(pl.multiple_of(h * dk, dk), dk)

    def load(h, slot):
        hbm, buf = ((k_hbm, k_buf), (v_hbm, v_buf), (q_hbm, q_buf))[slot]
        return pltpu.make_async_copy(hbm.at[:, columns(h)], buf.at[:, columns(h)], in_sem.at[slot, h])

    def store(h):
        return pltpu.make_async_copy(mix.at[:, columns(h)], mixed_hbm.at[:, columns(h)], out_sem.at[h])

    def piece(h, p):
        span = pl.ds(p * part, part)
        return pltpu.make_async_remote_copy(
            src_ref=outgoing.at[h, span], dst_ref=held.at[h, span],
            send_sem=send_sem.at[h, p], recv_sem=recv_sem.at[h, p],
            device_id={"seq": lax.rem(seq + 1, n_seq)}, device_id_type=MESH,
        )

    def start_loads(h, carry):
        for slot in range(3):
            load(h, slot).start()
        return carry

    lax.fori_loop(0, heads, start_loads, 0)

    @pl.when(seq == 0)
    def _():
        held[...] = jnp.zeros_like(held)

    squares[...] = jnp.zeros_like(squares)
    position = lax.broadcasted_iota(jnp.int32, (tokens, dk), 0).astype(F32)

    block = ROW_BLOCK if tokens % ROW_BLOCK == 0 else tokens
    tops = range(0, tokens, block)

    def prepare(h, carry, first=False):
        cols = columns(h)
        rate = jnp.full((1, dk), exps[h], jnp.int32).astype(F32) / (8.0 * tokens * n_seq)
        load(h, 0).wait()
        load(h, 1).wait()
        state = jnp.zeros((dk, dk), F32)
        for c, top in enumerate(tops):
            span = slice(top, top + block)
            scaled = (v_buf[span, cols].astype(F32) * jnp.exp2(position[span] * rate)).astype(BF16)
            v_buf[span, cols] = scaled
            running[h, c] = state
            state += dot(k_buf[span, cols], scaled, ((0,), (0,)))
        own = state * jnp.exp2(-rate * (tokens - 1.0))
        outgoing[h] = own
        for b in range(n_seq):
            final_rows[b, h] = own[b * rows : (b + 1) * rows]
        if first:
            pl.semaphore_wait(barrier, n_seq - 1 + n_group - 1)

        @pl.when(seq == 0)
        def _():
            for p in range(PIECES):
                piece(h, p).start()

        for b in range(last):

            @pl.when(b < seq)
            def _():
                pltpu.make_async_remote_copy(
                    src_ref=final_rows.at[b, h], dst_ref=late.at[seq, h],
                    send_sem=fin_send.at[b], recv_sem=fin_recv.at[seq],
                    device_id={"seq": b}, device_id_type=MESH,
                ).start()

        load(h, 2).wait()
        lower = lax.broadcasted_iota(jnp.int32, (block, block), 0) >= lax.broadcasted_iota(
            jnp.int32, (block, block), 1
        )
        for top in tops:
            span = slice(top, top + block)
            scores = dot(q_buf[span, cols], k_buf[span, cols], ((1,), (1,)))
            weights = jnp.where(lower, scores, 0.0).astype(BF16)
            mix[span, cols] = dot(weights, v_buf[span, cols], ((1,), (0,)))
        return carry

    def head_step(h, carry):
        cols = columns(h)
        rate = jnp.full((1, dk), exps[h], jnp.int32).astype(F32) / (8.0 * tokens * n_seq)
        block_decay = jnp.exp2(-rate * tokens)

        @pl.when(seq > 0)
        def _():
            for p in range(PIECES):
                span = pl.ds(p * part, part)
                piece(h, p).wait_recv()

                @pl.when(seq < last)
                def _():
                    outgoing[h, span] = outgoing[h, span] + held[h, span] * block_decay
                    piece(h, p).start()

        start = held[h] * jnp.exp2(-rate)
        for c, top in enumerate(tops):
            span = slice(top, top + block)
            inter = dot(q_buf[span, cols], (start + running[h, c]).astype(BF16), ((1,), (0,)))
            mixed = (mix[span, cols] + inter) * jnp.exp2(-(position[span] * rate))
            mix[span, cols] = mixed
            squares[span] += mixed * mixed
        store(h).start()

        @pl.when(h + lead < heads)
        def _():
            prepare(h + lead, 0)

        return carry

    lead = jnp.minimum(1 + LEAD * seq, heads)
    prepare(0, 0, first=True)
    lax.fori_loop(1, lead, prepare, 0)
    lax.fori_loop(0, heads, head_step, 0)

    sums[here] = jnp.broadcast_to(
        jnp.sum(squares[...].T, axis=0, keepdims=True), (8, padded)
    )

    def sum_copy(step, slot, target):
        return pltpu.make_async_remote_copy(
            src_ref=sums.at[slot], dst_ref=sums.at[slot],
            send_sem=sum_send.at[step], recv_sem=sum_recv.at[step],
            device_id={"head": target // n_sub, "sub": lax.rem(target, n_sub)},
            device_id_type=MESH,
        )

    for step in range(1, n_group):
        sum_copy(step, here, lax.rem(here + step, n_group)).start()
    for b in range(n_seq):

        @pl.when(seq == b)
        def _():
            for m in range(b + 1, n_seq):
                pltpu.make_async_copy(late.at[m], late.at[m], fin_recv.at[m]).wait()

            def finals(h, carry):
                rate = jnp.full((1, dk), exps[h], jnp.int32).astype(F32) / (8.0 * n_seq)
                total = held[h, b * rows : (b + 1) * rows] * jnp.exp2(-rate * (n_seq - b))
                total += final_rows[b, h] * jnp.exp2(-rate * (last - b))
                for m in range(b + 1, n_seq):
                    total += late[m, h] * jnp.exp2(-rate * (last - m))
                final[h] = total
                return carry

            lax.fori_loop(0, heads, finals, 0)

    final_copy = pltpu.make_async_copy(final, final_hbm, tail_sem.at[1])
    final_copy.start()
    for step in range(1, n_group):
        source = lax.rem(here - step + n_group, n_group)
        sum_copy(step, source, source).wait_recv()
    total = sums[0]
    for slot in range(1, n_group):
        total += sums[slot]
    factor = lax.rsqrt(total / (heads * dk * n_group) + 1e-06)
    inv[...] = jnp.broadcast_to(factor[:1], (dk, padded)).T[:tokens]
    inv_copy = pltpu.make_async_copy(inv, inv_hbm, tail_sem.at[0])
    inv_copy.start()

    for b in range(last):

        @pl.when(b < seq)
        def _():
            pltpu.make_async_copy(final_rows.at[b], final_rows.at[b], fin_send.at[b]).wait()

    @pl.when(seq < last)
    def _():
        def finish(h, carry):
            for p in range(PIECES):
                piece(h, p).wait_send()
            return carry

        lax.fori_loop(0, heads, finish, 0)

    for step in range(1, n_group):
        sum_copy(step, here, lax.rem(here + step, n_group)).wait_send()

    def stored(h, carry):
        store(h).wait()
        return carry

    lax.fori_loop(0, heads, stored, 0)
    inv_copy.wait()
    final_copy.wait()


def norm_kernel(heads, dk, mixed, inv, final, gain, normed_hbm, final_hbm, normed, sems):
    final_copy = pltpu.make_async_copy(final, final_hbm, sems.at[mixed.shape[0] // NORM_ROWS + 1])
    final_copy.start()

    tokens = mixed.shape[0]
    block = NORM_ROWS if tokens % NORM_ROWS == 0 else tokens

    def copy(n):
        span = pl.ds(n * block, block)
        return pltpu.make_async_copy(normed.at[span], normed_hbm.at[span], sems.at[n])

    for n in range(tokens // block):
        span = slice(n * block, (n + 1) * block)
        scale = inv[span]
        for h in range(heads):
            cols = slice(h * dk, (h + 1) * dk)
            normed[span, cols] = (mixed[span, cols] * scale * gain[:, cols]).astype(BF16)
        copy(n).start()
    for n in range(tokens // block):
        copy(n).wait()
    final_copy.wait()


def local(n_seq, n_head, n_sub, queries, keys, values, decay_exp, gain):
    tokens, features = queries.shape
    heads = decay_exp.shape[0]
    dk = features // heads
    rows = dk // n_seq
    padded = -(-tokens // 128) * 128
    n_group = n_head * n_sub
    hbm = pl.BlockSpec(memory_space=pl.ANY)
    mixed, inv, final = pl.pallas_call(
        functools.partial(mix_kernel, n_seq, n_head, n_sub, heads, dk),
        out_shape=(
            jax.ShapeDtypeStruct((tokens, features), F32),
            jax.ShapeDtypeStruct((tokens, dk), F32),
            jax.ShapeDtypeStruct((heads, rows, dk), F32),
        ),
        in_specs=[pl.BlockSpec(memory_space=pltpu.SMEM)] + [pl.BlockSpec(memory_space=pltpu.HBM)] * 3,
        out_specs=(hbm, hbm, hbm),
        scratch_shapes=[
            pltpu.VMEM((tokens, features), BF16),
            pltpu.VMEM((tokens, features), BF16),
            pltpu.VMEM((tokens, features), BF16),
            pltpu.VMEM((tokens, features), F32),
            pltpu.VMEM((heads, dk, dk), F32),
            pltpu.VMEM((heads, dk, dk), F32),
            pltpu.VMEM((n_seq, heads, rows, dk), F32),
            pltpu.VMEM((padded, dk), F32),
            pltpu.VMEM((n_group, 8, padded), F32),
            pltpu.VMEM((tokens, dk), F32),
            pltpu.VMEM((heads, max(1, tokens // ROW_BLOCK), dk, dk), F32),
            pltpu.VMEM((n_seq, heads, rows, dk), F32),
            pltpu.VMEM((heads, rows, dk), F32),
            pltpu.SemaphoreType.DMA((3, heads)),
            pltpu.SemaphoreType.DMA((heads,)),
            pltpu.SemaphoreType.DMA((heads, PIECES)),
            pltpu.SemaphoreType.DMA((heads, PIECES)),
            pltpu.SemaphoreType.DMA((n_seq,)),
            pltpu.SemaphoreType.DMA((n_seq,)),
            pltpu.SemaphoreType.DMA((n_group,)),
            pltpu.SemaphoreType.DMA((n_group,)),
            pltpu.SemaphoreType.DMA((2,)),
        ],
        compiler_params=pltpu.CompilerParams(
            collective_id=0, has_side_effects=True, vmem_limit_bytes=40 * 1024 * 1024
        ),
        name="mix",
    )(*(pltpu.with_memory_space_constraint(x, pltpu.HBM) for x in (decay_exp, queries, keys, values)))
    vmem = pl.BlockSpec(memory_space=pltpu.VMEM)
    return pl.pallas_call(
        functools.partial(norm_kernel, heads, dk),
        out_shape=(
            jax.ShapeDtypeStruct((tokens, features), BF16),
            jax.ShapeDtypeStruct((heads, rows, dk), F32),
        ),
        in_specs=[vmem] * 4,
        out_specs=(pl.BlockSpec(memory_space=pltpu.HBM),) * 2,
        scratch_shapes=[
            pltpu.VMEM((tokens, features), BF16),
            pltpu.SemaphoreType.DMA((tokens // NORM_ROWS + 2,)),
        ],
        compiler_params=pltpu.CompilerParams(vmem_limit_bytes=NORM_VMEM * 1024 * 1024),
        name="norm",
    )(
        *(pltpu.with_memory_space_constraint(x, pltpu.VMEM) for x in (mixed, inv, final)),
        gain.reshape(1, features),
    )


def solution(mesh):
    return jax.shard_map(
        functools.partial(local, mesh.shape["seq"], mesh.shape["head"], mesh.shape["sub"]),
        mesh=mesh,
        in_specs=(
            P(("groups", "seq"), ("head", "sub")),
            P(("groups", "seq"), ("head", "sub")),
            P(("groups", "seq"), ("head", "sub")),
            P(("head", "sub")),
            P(("head", "sub")),
        ),
        out_specs=(
            P(("groups", "seq"), ("head", "sub")),
            P(("groups", "head", "sub"), "seq", None),
        ),
        check_vma=False,
    )
```
